32 devices in a mesh: row: 16 (over z, y, x), feat: 2 (over core).
Axes of the slice: x: 2, y: 2, z: 4, core: 2. Of those that a mesh axis runs over, the one named last changes fastest.
Arguments:
- codes: int32 [8192, 2048], P('row', 'feat'), may hold values from 0 to 255
- nodes: int32 [8192], P('row'), may hold values from 0 to 3
- labels: int32 [8192], P('row'), may hold values 0 or 1
- weights: float32 [2048], P('feat'), may hold values from -0.125 to 0.125
Outputs:
- gain: float32 [4, 2048, 256], P(None, ('feat', 'row'))
The draws below stay inside these ranges and needn't reach their ends.
All inputs are finite; a program needn't handle non-finite values. No bound on the sum of `labels` on one device may be relied on, other than what follows from the above.
Results may differ from the reference program's by a relative error of at most 0.0047.
Values sent between devices are 32-bit elements; how exact they have to be, the bound alone decides.
A program may use at most 64 MiB of HBM per device.

```python
import math
import jax
import jax.numpy as jnp
from jax import lax

F = 2048
BINS = 256
NODES = 4
ROWS = 8192


def plant(result, stream_key, low, largest):
    dims = result.shape
    spot = [jax.random.randint(jax.random.fold_in(stream_key, axis), (), 0, dims[axis]) for axis in range(len(dims))]
    result = result.at[tuple(spot)].set(low)
    longest = dims.index(max(dims))
    spot[longest] = (spot[longest] + 1) % dims[longest]
    return result.at[tuple(spot)].set(largest)


def steps_of(key, extent, cuts, least, top_value):
    def one(position, blocks):
        heights = jax.random.uniform(jax.random.fold_in(jax.random.fold_in(key, 6), position), (blocks,), jnp.float32, least / len(cuts), top_value / len(cuts))
        return jnp.repeat(jnp.exp(heights), extent[position] // blocks).reshape((-1,) + (1,) * (len(extent) - position - 1))

    loudness = one(*cuts[0])
    for cut in cuts[1:]:
        loudness = loudness * one(*cut)
    return loudness


def centred(key, dims, spread, bound, shards=(), kind=jnp.bfloat16):
    loudness = steps_of(key, dims, shards, -0.22, 0.18) if shards else 1.0
    result = jax.random.normal(key, dims, jnp.float32) * spread * loudness
    return jnp.minimum(jnp.maximum(result, -bound), bound).astype(kind)


def setup_inputs(seed: int = 0) -> dict:
    splits = jax.random.split(jax.random.key(seed), 5)
    return {
        "codes": plant(jax.random.randint(splits[0], (ROWS, F), 0, BINS), jax.random.fold_in(splits[0], 1), 0, BINS - 1).astype(jnp.int32),
        "nodes": plant(jax.random.randint(splits[1], (ROWS,), 0, NODES), jax.random.fold_in(splits[1], 1), 0, NODES - 1).astype(jnp.int32),
        "labels": plant((jax.random.randint(splits[2], (ROWS,), 0, 4) < 1).astype(jnp.int32), jax.random.fold_in(splits[2], 1), 0, 1),
        "weights": centred(splits[3], (F,), F ** -0.5, 0.125, ((0, 2),), jnp.float32),
    }


def reference(codes, nodes, labels, weights):
    value = (codes.astype(jnp.float32) - (BINS - 1) / 2.0) * (2.0 / BINS)
    margin = jnp.dot(value, weights, precision=lax.Precision.HIGHEST)
    prob = 1.0 / (1.0 + jnp.exp(-margin))
    grad = prob - labels.astype(jnp.float32)
    hess = prob * (1.0 - prob)
    member = (nodes[:, None] == jnp.arange(NODES, dtype=jnp.int32)[None, :]).astype(jnp.float32)
    stats = jnp.concatenate([member * grad[:, None], member * hess[:, None]], axis=1).astype(jnp.bfloat16)
    wide = stats.astype(jnp.float32)
    block = math.gcd(F, 16)
    grouped = jnp.transpose(codes.reshape(ROWS, F // block, block), (1, 0, 2))
    offsets = (jnp.arange(block, dtype=jnp.int32) * BINS)[None, :]

    def one_block(code_block):
        ids = (code_block + offsets).reshape(-1)
        data = jnp.broadcast_to(wide[:, None, :], (ROWS, block, 2 * NODES)).reshape(-1, 2 * NODES)
        summed = jax.ops.segment_sum(data, ids, num_segments=block * BINS)
        return summed.reshape(block, BINS, 2 * NODES)

    hist = lax.map(one_block, grouped).reshape(F, BINS, 2 * NODES)
    total = jnp.sum(wide, axis=0)
    left = jnp.cumsum(hist, axis=1)
    grad_left = left[:, :, :NODES]
    hess_left = left[:, :, NODES:]
    grad_total = total[:NODES][None, None, :]
    hess_total = total[NODES:][None, None, :]
    lam = 1.0
    gain = 0.5 * (grad_left * grad_left / (hess_left + lam)
                  + (grad_total - grad_left) ** 2 / (hess_total - hess_left + lam)
                  - grad_total * grad_total / (hess_total + lam))
    return jnp.transpose(gain, (2, 0, 1))
```

```python
import functools
import math

import jax
import jax.numpy as jnp
from jax import lax
from jax.experimental import pallas as pl
from jax.experimental.pallas import tpu as pltpu
from jax.sharding import PartitionSpec as P

BINS = 256
NODES = 4
STATS = 2 * NODES
HIGH = 4
LOW = BINS // HIGH
TILE = 16
LANES = 128
AHEAD = 3


def kernel(
    halves,
    inner,
    feats,
    turn,
    given_ref,
    weights_ref,
    nodes_ref,
    labels_ref,
    gain_ref,
    raw_ref,
    turned_ref,
    margin_ref,
    code_buf,
    margin_buf,
    stat_buf,
    high_ref,
    low_ref,
    acc_ref,
    left_ref,
    peer_ref,
    raw_sem,
    own_sem,
    code_send,
    code_recv,
    margin_send,
    margin_recv,
    stat_send,
    stat_recv,
    left_send,
    left_recv,
):
    parts, size, rows = turned_ref.shape[1:] if turn else given_ref.shape[1:]
    codes_ref = turned_ref if turn else given_ref
    chunks = halves * parts
    batch = math.gcd(inner, 4)
    me_row = lax.axis_index("row")
    me_feat = lax.axis_index("feat")
    me_out = me_row // inner
    me_in = me_row % inner

    def peer(k):
        return me_out * inner + (me_in + k) % inner

    partner = ((me_out + 1) % halves) * inner + me_in

    def owner(chunk, k):
        half = (me_out + halves - 1 - chunk // parts) % halves
        return half * inner + (me_in + k) % inner

    def code_copy(chunk, k):
        return pltpu.make_async_remote_copy(
            src_ref=codes_ref.at[owner(chunk, k), chunk % parts],
            dst_ref=code_buf.at[chunk, k],
            send_sem=code_send.at[chunk, k],
            recv_sem=code_recv.at[chunk, k],
            device_id={"row": peer(k)},
            device_id_type=pl.DeviceIdType.MESH,
        )

    def own_copy(chunk):
        return pltpu.make_async_copy(
            codes_ref.at[owner(chunk, 0), chunk % parts], code_buf.at[chunk, 0], own_sem.at[chunk]
        )

    def margin_copy(k):
        return pltpu.make_async_remote_copy(
            src_ref=margin_ref,
            dst_ref=margin_buf.at[k],
            send_sem=margin_send.at[k],
            recv_sem=margin_recv.at[k],
            device_id={"feat": (me_feat + k) % feats},
            device_id_type=pl.DeviceIdType.MESH,
        )

    def stat_copy(k):
        return pltpu.make_async_remote_copy(
            src_ref=stat_buf.at[0],
            dst_ref=stat_buf.at[k],
            send_sem=stat_send.at[k],
            recv_sem=stat_recv.at[k],
            device_id={"row": peer(k)},
            device_id_type=pl.DeviceIdType.MESH,
        )

    def left_copy(chunk):
        return pltpu.make_async_remote_copy(
            src_ref=left_ref.at[chunk],
            dst_ref=peer_ref.at[chunk],
            send_sem=left_send.at[chunk],
            recv_sem=left_recv.at[chunk],
            device_id={"row": partner},
            device_id_type=pl.DeviceIdType.MESH,
        )

    def each(low, high, body):
        def step(i, carry):
            body(i)
            return carry

        lax.fori_loop(low, high, step, 0)

    if turn:
        blocks = raw_ref.shape[0]
        per = LANES // (parts * size)
        first_block = ((me_out + halves - 1) % halves) * (blocks // halves)

        def raw_copy(t):
            column = pl.multiple_of((first_block + t) % blocks * LANES, LANES)
            return pltpu.make_async_copy(
                given_ref.at[:, pl.ds(column, LANES)], raw_ref.at[t], raw_sem.at[t]
            )

        for t in range(blocks):
            raw_copy(t).start()
        part = [jnp.zeros((1, rows), jnp.float32)]

        def turn_block(t):
            raw_copy(t).wait()
            turned = jnp.transpose(raw_ref[t].astype(jnp.float32))
            block = (first_block + t) % blocks
            turned_ref[pl.ds(block * per, per)] = turned.reshape(per, parts, size, rows)
            centred = (turned - (BINS - 1) / 2.0).astype(jnp.bfloat16)
            weight = weights_ref[:, pl.ds(pl.multiple_of(block * LANES, LANES), LANES)]
            coarse = weight.astype(jnp.bfloat16).astype(jnp.float32)
            rest = weight - coarse
            middle = rest.astype(jnp.bfloat16).astype(jnp.float32)
            line = lax.broadcasted_iota(jnp.int32, (TILE, LANES), 0)
            split = jnp.where(
                line == 0,
                coarse,
                jnp.where(line == 1, middle, jnp.where(line == 2, rest - middle, 0.0)),
            ).astype(jnp.bfloat16)
            product = jnp.dot(split, centred, preferred_element_type=jnp.float32)
            part[0] = part[0] + (product[0:1] + (product[1:2] + product[2:3])) * (2.0 / BINS)

    barrier = pltpu.get_barrier_semaphore()
    each(
        1,
        inner,
        lambda k: pl.semaphore_signal(
            barrier, inc=1, device_id={"row": peer(k)}, device_id_type=pl.DeviceIdType.MESH
        ),
    )
    each(
        1,
        feats,
        lambda k: pl.semaphore_signal(
            barrier,
            inc=1,
            device_id={"feat": (me_feat + k) % feats},
            device_id_type=pl.DeviceIdType.MESH,
        ),
    )
    if halves > 1:
        pl.semaphore_signal(
            barrier, inc=1, device_id={"row": partner}, device_id_type=pl.DeviceIdType.MESH
        )

    def barrier_wait():
        pl.semaphore_wait(barrier, inner - 1 + feats - 1 + halves - 1)

    def send_chunk(chunk):
        own_copy(chunk).start()
        each(1, inner, lambda k: code_copy(chunk, k).start())

    if turn:
        for t in range(blocks // halves):
            turn_block(t)
        barrier_wait()
        send_chunk(0)
        for t in range(blocks // halves, blocks):
            turn_block(t)
        margin_ref[...] = part[0]
    else:
        margin_ref[...] = weights_ref[...]
        barrier_wait()
        send_chunk(0)
    each(1, feats, lambda k: margin_copy(k).start())
    margin = margin_ref[...]
    for k in range(1, feats):
        margin_copy(k).wait_recv()
        margin = margin + margin_buf[k]
    prob = 1.0 / (1.0 + jnp.exp(-margin))
    grad = prob - labels_ref[...].astype(jnp.float32)
    hess = prob * (1.0 - prob)
    node = lax.broadcasted_iota(jnp.int32, (NODES, rows), 0)
    member = (nodes_ref[...] == node).astype(jnp.float32)
    stat_buf[0] = jnp.concatenate([member * grad, member * hess], 0)
    each(1, inner, lambda k: stat_copy(k).start())
    for chunk in range(1, AHEAD):
        send_chunk(chunk)
    each(1, inner, lambda k: stat_copy(k).wait_recv())

    sub = lax.broadcasted_iota(jnp.int32, (TILE, rows), 0)
    high_id = (sub // STATS).astype(jnp.float32).astype(jnp.bfloat16)
    low_id = sub.astype(jnp.float32).astype(jnp.bfloat16)
    zero = jnp.zeros((TILE, rows), jnp.bfloat16)
    one = jnp.ones((TILE, rows), jnp.bfloat16)

    def chunk_step(chunk):
        @pl.when(chunk + AHEAD < chunks)
        def _():
            send_chunk(chunk + AHEAD)

        acc_ref[...] = jnp.zeros_like(acc_ref)
        own_copy(chunk).wait()

        def batch_step(j):
            first = j * batch
            for q in range(batch):
                if q == 0:
                    @pl.when(j > 0)
                    def _():
                        code_copy(chunk, first).wait_recv()
                else:
                    code_copy(chunk, first + q).wait_recv()
                codes = code_buf[chunk, first + q]
                high = jnp.floor(codes * (1.0 / LOW))
                high_ref[q] = high
                low_ref[q] = codes - high * LOW
            stats = []
            for q in range(batch):
                s = stat_buf[first + q]
                stats.append(jnp.concatenate([s] * (TILE // STATS), 0).astype(jnp.bfloat16))
            for f in range(size):
                aa, bb = [], []
                for q in range(batch):
                    h = jnp.broadcast_to(high_ref[q, f : f + 1, :], (TILE, rows)).astype(jnp.bfloat16)
                    l = jnp.broadcast_to(low_ref[q, f : f + 1, :], (TILE, rows)).astype(jnp.bfloat16)
                    aa.append(
                        jnp.concatenate(
                            [
                                jnp.where(h == high_id + jnp.bfloat16(i * (TILE // STATS)), stats[q], zero)
                                for i in range(HIGH * STATS // TILE)
                            ],
                            0,
                        )
                    )
                    bb.append(
                        jnp.concatenate(
                            [
                                jnp.where(l <= low_id + jnp.bfloat16(i * TILE), one, zero)
                                for i in range(LOW // TILE)
                            ],
                            0,
                        )
                    )
                acc_ref[f] += lax.dot_general(
                    jnp.concatenate(aa, 1),
                    jnp.concatenate(bb, 1),
                    (((1,), (1,)), ((), ())),
                    preferred_element_type=jnp.float32,
                )

        each(0, inner // batch, batch_step)
        for f in range(size):
            acc = acc_ref[f]
            total = jnp.zeros((STATS, 1), jnp.float32)
            pieces = []
            for h in range(HIGH):
                piece = acc[h * STATS : (h + 1) * STATS] + total
                pieces.append(piece)
                total = piece[:, LOW - 1 : LOW]
            left_ref[chunk, f] = jnp.concatenate(pieces, 1)

        if halves > 1:
            @pl.when(chunk < parts)
            def _():
                left_copy(chunk).start()

    each(0, chunks, chunk_step)

    for c in range(parts):
        if halves > 1:
            left_copy(c).wait_recv()
        lam = 1.0
        paired = size % 2 == 0
        for f in range(0, size, 2 if paired else 1):
            grads, hesses = [], []
            for g in range(f, f + 2 if paired else f + 1):
                left = left_ref[chunks - parts + c, g]
                if halves > 1:
                    left = left + peer_ref[c, g]
                grads.append(left[:NODES])
                hesses.append(left[NODES:])
            gl = jnp.concatenate(grads, 0)
            hl = jnp.concatenate(hesses, 0)
            gt, ht = gl[:, BINS - 1 : BINS], hl[:, BINS - 1 : BINS]
            gain = 0.5 * (
                gl * gl / (hl + lam) + (gt - gl) ** 2 / (ht - hl + lam) - gt * gt / (ht + lam)
            )
            for g in range(len(grads)):
                gain_ref[:, c * size + f + g, :] = gain[g * NODES : (g + 1) * NODES]

    each(1, feats, lambda k: margin_copy(k).wait_send())
    each(1, inner, lambda k: stat_copy(k).wait_send())
    each(0, chunks, lambda c: each(1, inner, lambda k: code_copy(c, k).wait_send()))
    if halves > 1:
        each(0, parts, lambda c: left_copy(c).wait_send())


def shards(codes, nodes, labels, weights):
    row_count, feat_count = codes.shape
    groups = lax.axis_size("row")
    feats = lax.axis_size("feat")
    owned = feat_count // groups
    halves = math.gcd(groups, 2)
    inner = groups // halves
    parts = math.gcd(owned, 4)
    size = owned // parts
    turn = size % 8 == 0 and LANES % owned == 0 and feat_count % (LANES * halves) == 0
    if turn:
        given, vector = codes, weights[None, :]
    else:
        value = (codes.astype(jnp.float32) - (BINS - 1) / 2.0) * (2.0 / BINS)
        vector = jnp.dot(value, weights, precision=lax.Precision.HIGHEST)[None, :]
        given = codes.T.reshape(groups, parts, size, row_count).astype(jnp.float32)
    blocks = feat_count // LANES if turn else 1
    chunks = halves * parts
    batch = math.gcd(inner, 4)
    dma = pltpu.SemaphoreType.DMA
    return pl.pallas_call(
        functools.partial(kernel, halves, inner, feats, turn),
        in_specs=[pl.BlockSpec(memory_space=pl.ANY if turn else pltpu.VMEM)]
        + [pl.BlockSpec(memory_space=pltpu.VMEM)] * 3,
        out_specs=pl.BlockSpec(memory_space=pltpu.VMEM),
        out_shape=jax.ShapeDtypeStruct((NODES, owned, BINS), jnp.float32),
        scratch_shapes=[
            pltpu.VMEM((blocks, row_count, LANES) if turn else (1, 8, LANES), jnp.int32),
            pltpu.VMEM((groups, parts, size, row_count) if turn else (1, 1, 8, LANES), jnp.float32),
            pltpu.VMEM((1, row_count), jnp.float32),
            pltpu.VMEM((chunks, inner, size, row_count), jnp.float32),
            pltpu.VMEM((feats, 1, row_count), jnp.float32),
            pltpu.VMEM((inner, STATS, row_count), jnp.float32),
            pltpu.VMEM((batch, size, row_count), jnp.float32),
            pltpu.VMEM((batch, size, row_count), jnp.float32),
            pltpu.VMEM((size, HIGH * STATS, LOW), jnp.float32),
            pltpu.VMEM((chunks, size, STATS, BINS), jnp.float32),
            pltpu.VMEM((parts, size, STATS, BINS), jnp.float32),
            dma((blocks,)),
            dma((chunks,)),
            dma((chunks, inner)),
            dma((chunks, inner)),
            dma((feats,)),
            dma((feats,)),
            dma((inner,)),
            dma((inner,)),
            dma((parts,)),
            dma((parts,)),
        ],
        compiler_params=pltpu.CompilerParams(collective_id=0, has_side_effects=True),
    )(given, vector, nodes[None, :], labels[None, :])


PLANES = 4
CHUNK = 8
EARLY = 2
AHEAD_PLANE = 6
DELAY_INNER_AWAY = 4
DELAY_INNER_HOME = 9
DELAY_OUTER_HOME = 13


def plane_kernel(
    n,
    feats,
    early,
    given_ref,
    weights_ref,
    nodes_ref,
    labels_ref,
    gain_ref,
    raw_ref,
    turned_ref,
    margin_ref,
    code_buf,
    margin_buf,
    stat_buf,
    high_ref,
    low_ref,
    hist_buf,
    come_buf,
    gain_own,
    gain_out,
    gain_in,
    raw_sem,
    own_sem,
    code_send,
    code_recv,
    margin_send,
    margin_recv,
    stat_send,
    stat_recv,
    hist_send,
    hist_recv,
    gain_send,
    gain_recv,
    out_sem,
):
    parts, size, rows = turned_ref.shape[1:]
    blocks = raw_ref.shape[0]
    per = LANES // (parts * size)
    block_span = n // per
    steps = 4 * parts
    me_row = lax.axis_index("row")
    me_feat = lax.axis_index("feat")
    plane = me_row // n
    me_in = me_row % n
    half = plane // 2
    inner_plane = 1 + half
    outer_plane = 3 * half
    outer = plane == outer_plane
    inner = plane == inner_plane

    def each(low, high, body):
        def step(i, carry):
            body(i)
            return carry

        lax.fori_loop(low, high, step, 0)

    def spot(k):
        return (me_in + k) % n

    def away(i):
        return i % 2 == 0

    def is_early(i):
        return jnp.logical_and(away(i), i // 2 < early)

    def group_of(i):
        base = jnp.where(i // 2 < parts, inner_plane, outer_plane)
        return jnp.where(away(i), PLANES - 1 - base, base)

    def part_of(i):
        return (i // 2) % parts

    def remote(src, dst, send, recv, row):
        return pltpu.make_async_remote_copy(
            src_ref=src,
            dst_ref=dst,
            send_sem=send,
            recv_sem=recv,
            device_id={"row": row},
            device_id_type=pl.DeviceIdType.MESH,
        )

    def code_copy(i, k):
        return remote(
            turned_ref.at[group_of(i) * n + spot(k), part_of(i)],
            code_buf.at[i, k],
            code_send.at[i, k],
            code_recv.at[i, k],
            plane * n + spot(k),
        )

    def early_copy(i, k):
        slot = steps + i // 2
        return remote(
            turned_ref.at[group_of(i) * n + spot(k), part_of(i)],
            code_buf.at[slot, k],
            code_send.at[slot, k],
            code_recv.at[slot, k],
            inner_plane * n + spot(k),
        )

    def own_copy(i):
        return pltpu.make_async_copy(
            turned_ref.at[group_of(i) * n + me_in, part_of(i)], code_buf.at[i, 0], own_sem.at[i]
        )

    def margin_copy(k):
        return pltpu.make_async_remote_copy(
            src_ref=margin_ref,
            dst_ref=margin_buf.at[k],
            send_sem=margin_send.at[k],
            recv_sem=margin_recv.at[k],
            device_id={"feat": (me_feat + k) % feats},
            device_id_type=pl.DeviceIdType.MESH,
        )

    def stat_copy(k):
        return remote(
            stat_buf.at[0], stat_buf.at[k], stat_send.at[k], stat_recv.at[k], plane * n + spot(k)
        )

    def stat_in_copy(k):
        return remote(
            stat_buf.at[0],
            stat_buf.at[n + k],
            stat_send.at[n + k],
            stat_recv.at[n + k],
            inner_plane * n + spot(k),
        )

    def hist_copy(i):
        far = jnp.where(outer, inner_plane, jnp.where(away(i), PLANES - 1 - plane, outer_plane))
        there = jnp.where(jnp.logical_and(inner, away(i)), i + 1, i)
        return remote(
            hist_buf.at[i], come_buf.at[there], hist_send.at[i], hist_recv.at[there], far * n + me_in
        )

    def gain_copy(c):
        return remote(
            gain_out.at[c], gain_in.at[c], gain_send.at[c], gain_recv.at[c], inner_plane * n + me_in
        )

    def out_copy(src, c):
        row = pl.multiple_of(c * size, size)
        return pltpu.make_async_copy(
            src.at[c], gain_ref.at[:, pl.ds(row, size), :], out_sem.at[c]
        )

    order = [
        PLANES - 1 - inner_plane,
        inner_plane,
        PLANES - 1 - outer_plane,
        outer_plane,
    ]

    def block_of(t):
        return order[t // block_span] * block_span + t % block_span

    def raw_copy(t):
        column = pl.multiple_of(block_of(t) * LANES, LANES)
        return pltpu.make_async_copy(
            given_ref.at[:, pl.ds(column, LANES)], raw_ref.at[t], raw_sem.at[t]
        )

    for t in range(blocks):
        raw_copy(t).start()

    barrier = pltpu.get_barrier_semaphore()

    def greet(row):
        pl.semaphore_signal(
            barrier, inc=1, device_id={"row": row}, device_id_type=pl.DeviceIdType.MESH
        )

    each(1, n, lambda k: greet(plane * n + spot(k)))
    facing = jnp.where(outer, inner_plane, outer_plane)
    each(0, n, lambda k: greet(facing * n + spot(k)))

    @pl.when(inner)
    def _():
        greet((PLANES - 1 - plane) * n + me_in)

    each(
        1,
        feats,
        lambda k: pl.semaphore_signal(
            barrier,
            inc=1,
            device_id={"feat": (me_feat + k) % feats},
            device_id_type=pl.DeviceIdType.MESH,
        ),
    )

    def send_chunk(i):
        relayed = jnp.logical_and(outer, is_early(i))

        @pl.when(relayed)
        def _():
            each(0, n, lambda k: early_copy(i, k).start())

        @pl.when(jnp.logical_not(relayed))
        def _():
            own_copy(i).start()
            each(1, n, lambda k: code_copy(i, k).start())

    part_sum = [jnp.zeros((1, rows), jnp.float32)]

    def turn_block(t):
        raw_copy(t).wait()
        turned = jnp.transpose(raw_ref[t].astype(jnp.float32))
        block = block_of(t)
        turned_ref[pl.ds(block * per, per)] = turned.reshape(per, parts, size, rows)
        centred = (turned - (BINS - 1) / 2.0).astype(jnp.bfloat16)
        weight = weights_ref[:, pl.ds(pl.multiple_of(block * LANES, LANES), LANES)]
        coarse = weight.astype(jnp.bfloat16).astype(jnp.float32)
        rest = weight - coarse
        middle = rest.astype(jnp.bfloat16).astype(jnp.float32)
        line = lax.broadcasted_iota(jnp.int32, (TILE, LANES), 0)
        split = jnp.where(
            line == 0,
            coarse,
            jnp.where(line == 1, middle, jnp.where(line == 2, rest - middle, 0.0)),
        ).astype(jnp.bfloat16)
        product = jnp.dot(split, centred, preferred_element_type=jnp.float32)
        part_sum[0] = part_sum[0] + (
            product[0:1] + (product[1:2] + product[2:3])
        ) * (2.0 / BINS)

    for t in range(block_span):
        turn_block(t)
    pl.semaphore_wait(barrier, jnp.where(outer, 2 * n - 1, 2 * n) + feats - 1)
    each(0, early, lambda a: send_chunk(2 * a))
    for t in range(block_span, blocks):
        turn_block(t)
    margin_ref[...] = part_sum[0]
    each(1, feats, lambda k: margin_copy(k).start())
    each(0, early, lambda a: send_chunk(2 * a + 1))
    margin = margin_ref[...]
    for k in range(1, feats):
        margin_copy(k).wait_recv()
        margin = margin + margin_buf[k]
    prob = 1.0 / (1.0 + jnp.exp(-margin))
    grad = prob - labels_ref[...].astype(jnp.float32)
    hess = prob * (1.0 - prob)
    node = lax.broadcasted_iota(jnp.int32, (NODES, rows), 0)
    member = (nodes_ref[...] == node).astype(jnp.float32)
    stat_buf[0] = jnp.concatenate([member * grad, member * hess], 0)
    each(1, n, lambda k: stat_copy(k).start())

    @pl.when(outer)
    def _():
        each(0, n, lambda k: stat_in_copy(k).start())

    each(2 * early, AHEAD_PLANE, send_chunk)
    each(1, n, lambda k: stat_copy(k).wait_recv())

    @pl.when(inner)
    def _():
        each(0, n, lambda k: stat_in_copy(k).wait_recv())

    sub = lax.broadcasted_iota(jnp.int32, (TILE, rows), 0)
    high_id = (sub // STATS).astype(jnp.float32).astype(jnp.bfloat16)
    low_id = sub.astype(jnp.float32).astype(jnp.bfloat16)
    zero = jnp.zeros((TILE, rows), jnp.bfloat16)
    one = jnp.ones((TILE, rows), jnp.bfloat16)
    front = lax.broadcasted_iota(jnp.int32, (STATS, LANES), 1) < LOW
    front_all = lax.broadcasted_iota(jnp.int32, (HIGH * STATS, LANES), 1) < LOW

    def compute(i):
        hist_buf[i] = jnp.zeros(hist_buf.shape[1:], jnp.float32)

        def batch_step(b):
            slot = jnp.where(b == 0, i, steps + i // 2)
            for q in range(n):
                if q == 0:
                    @pl.when(b == 0)
                    def _():
                        own_copy(i).wait()

                    @pl.when(b > 0)
                    def _():
                        early_copy(i, 0).wait_recv()
                else:
                    remote(
                        turned_ref.at[0, 0],
                        code_buf.at[slot, q],
                        code_send.at[slot, q],
                        code_recv.at[slot, q],
                        plane * n + spot(q),
                    ).wait_recv()
                codes = code_buf[slot, q]
                high = jnp.floor(codes * (1.0 / LOW))
                high_ref[q] = high
                low_ref[q] = codes - high * LOW
            stats = []
            for q in range(n):
                s = stat_buf[b * n + q]
                stats.append(jnp.concatenate([s] * (TILE // STATS), 0).astype(jnp.bfloat16))
            for p in range(size // 2):
                aa, bb = [], []
                for q in range(n):
                    a_rows, b_rows = [], []
                    for f in (2 * p, 2 * p + 1):
                        h = jnp.broadcast_to(high_ref[q, f : f + 1, :], (TILE, rows)).astype(jnp.bfloat16)
                        l = jnp.broadcast_to(low_ref[q, f : f + 1, :], (TILE, rows)).astype(jnp.bfloat16)
                        for t in range(HIGH * STATS // TILE):
                            a_rows.append(
                                jnp.where(h == high_id + jnp.bfloat16(t * (TILE // STATS)), stats[q], zero)
                            )
                        for t in range(LOW // TILE):
                            b_rows.append(jnp.where(l <= low_id + jnp.bfloat16(t * TILE), one, zero))
                    aa.append(jnp.concatenate(a_rows, 0))
                    bb.append(jnp.concatenate(b_rows, 0))
                both = lax.dot_general(
                    jnp.concatenate(aa, 1),
                    jnp.concatenate(bb, 1),
                    (((1,), (1,)), ((), ())),
                    preferred_element_type=jnp.float32,
                )
                hist_buf[i, p] += jnp.where(
                    front_all, both[: HIGH * STATS], both[HIGH * STATS :]
                )

        each(0, jnp.where(jnp.logical_and(inner, is_early(i)), 2, 1), batch_step)

    def finalise(i, target):
        lam = 1.0
        c = part_of(i)
        for p in range(size // 2):
            total = jnp.zeros((STATS, LANES), jnp.float32)
            lines = []
            for h in range(HIGH):
                piece = (
                    hist_buf[i, p, h * STATS : (h + 1) * STATS]
                    + come_buf[i, p, h * STATS : (h + 1) * STATS]
                )
                lines.append(piece + total)
                if h + 1 < HIGH:
                    total = total + jnp.where(
                        front, piece[:, LOW - 1 : LOW], piece[:, 2 * LOW - 1 : 2 * LOW]
                    )
            rolled = [pltpu.roll(line, LOW, 1) for line in lines]
            lefts = [
                jnp.concatenate(
                    [jnp.where(front, lines[0], rolled[1]), jnp.where(front, lines[2], rolled[3])], 1
                ),
                jnp.concatenate(
                    [jnp.where(front, rolled[0], lines[1]), jnp.where(front, rolled[2], lines[3])], 1
                ),
            ]
            gl = jnp.concatenate([left[:NODES] for left in lefts], 0)
            hl = jnp.concatenate([left[NODES:] for left in lefts], 0)
            gt, ht = gl[:, BINS - 1 : BINS], hl[:, BINS - 1 : BINS]
            gain = 0.5 * (
                gl * gl / (hl + lam) + (gt - gl) ** 2 / (ht - hl + lam) - gt * gt / (ht + lam)
            )
            for g in range(2):
                target[c, :, 2 * p + g, :] = gain[g * NODES : (g + 1) * NODES]

    def settle(i):
        hist_copy_in = remote(
            hist_buf.at[i], come_buf.at[i], hist_send.at[i], hist_recv.at[i], plane * n + spot(1)
        )
        hist_copy_in.wait_recv()

        @pl.when(inner)
        def _():
            hist_buf[i] += come_buf[i]
            hist_copy(i).start()

    delay_home = jnp.where(outer, DELAY_OUTER_HOME, DELAY_INNER_HOME)

    def step(t):
        @pl.when(t < steps)
        def _():
            @pl.when(t + AHEAD_PLANE < steps)
            def _():
                send_chunk(t + AHEAD_PLANE)

            @pl.when(jnp.logical_not(jnp.logical_and(outer, is_early(t))))
            def _():
                compute(t)

            @pl.when(jnp.logical_and(away(t), is_early(t) == inner))
            def _():
                hist_copy(t).start()

        i = t - DELAY_INNER_AWAY

        @pl.when(
            jnp.logical_and(
                jnp.logical_and(inner, jnp.logical_and(i >= 2 * early, i < steps)), i % 2 == 0
            )
        )
        def _():
            settle(i)

        j = t - delay_home

        @pl.when(jnp.logical_and(jnp.logical_and(j >= 0, j < steps), j % 2 == 1))
        def _():
            settle(j)

            @pl.when(jnp.logical_and(outer, j // 2 < parts))
            def _():
                finalise(j, gain_out)
                gain_copy(part_of(j)).start()

            @pl.when(jnp.logical_and(outer, j // 2 >= parts))
            def _():
                finalise(j, gain_own)
                out_copy(gain_own, part_of(j)).start()

    each(0, steps + max(DELAY_INNER_AWAY, DELAY_INNER_HOME, DELAY_OUTER_HOME), step)

    @pl.when(inner)
    def _():
        def take(c):
            gain_copy(c).wait_recv()
            out_copy(gain_in, c).start()

        each(0, parts, take)

    each(1, feats, lambda k: margin_copy(k).wait_send())
    each(1, n, lambda k: stat_copy(k).wait_send())

    @pl.when(outer)
    def _():
        each(0, n, lambda k: stat_in_copy(k).wait_send())
        each(0, parts, lambda c: gain_copy(c).wait_send())
        each(0, early, lambda a: each(0, n, lambda k: early_copy(2 * a, k).wait_send()))

    def finish(i):
        @pl.when(jnp.logical_not(jnp.logical_and(outer, is_early(i))))
        def _():
            each(1, n, lambda k: code_copy(i, k).wait_send())

        @pl.when(jnp.logical_or(inner, jnp.logical_and(away(i), jnp.logical_not(is_early(i)))))
        def _():
            hist_copy(i).wait_send()

    each(0, steps, finish)

    each(0, parts, lambda c: out_copy(gain_own, c).wait())


def plane_shards(codes, nodes, labels, weights):
    row_count, feat_count = codes.shape
    groups = lax.axis_size("row")
    feats = lax.axis_size("feat")
    owned = feat_count // groups
    n = groups // PLANES
    size = CHUNK
    parts = owned // size
    blocks = feat_count // LANES
    steps = 4 * parts
    early = min(EARLY, parts)
    dma = pltpu.SemaphoreType.DMA
    return pl.pallas_call(
        functools.partial(plane_kernel, n, feats, early),
        in_specs=[pl.BlockSpec(memory_space=pl.ANY)]
        + [pl.BlockSpec(memory_space=pltpu.VMEM)] * 3,
        out_specs=pl.BlockSpec(memory_space=pl.ANY),
        out_shape=jax.ShapeDtypeStruct((NODES, owned, BINS), jnp.float32),
        scratch_shapes=[
            pltpu.VMEM((blocks, row_count, LANES), jnp.int32),
            pltpu.VMEM((groups, parts, size, row_count), jnp.float32),
            pltpu.VMEM((1, row_count), jnp.float32),
            pltpu.VMEM((steps + early, n, size, row_count), jnp.float32),
            pltpu.VMEM((feats, 1, row_count), jnp.float32),
            pltpu.VMEM((2 * n, STATS, row_count), jnp.float32),
            pltpu.VMEM((n, size, row_count), jnp.float32),
            pltpu.VMEM((n, size, row_count), jnp.float32),
            pltpu.VMEM((steps, size // 2, HIGH * STATS, LANES), jnp.float32),
            pltpu.VMEM((steps, size // 2, HIGH * STATS, LANES), jnp.float32),
            pltpu.VMEM((parts, NODES, size, BINS), jnp.float32),
            pltpu.VMEM((parts, NODES, size, BINS), jnp.float32),
            pltpu.VMEM((parts, NODES, size, BINS), jnp.float32),
            dma((blocks,)),
            dma((steps,)),
            dma((steps + early, n)),
            dma((steps + early, n)),
            dma((feats,)),
            dma((feats,)),
            dma((2 * n,)),
            dma((2 * n,)),
            dma((steps,)),
            dma((steps,)),
            dma((parts,)),
            dma((parts,)),
            dma((parts,)),
        ],
        compiler_params=pltpu.CompilerParams(collective_id=0, has_side_effects=True),
    )(codes, weights[None, :], nodes[None, :], labels[None, :])


def fits(mesh, codes):
    groups, feats = mesh.shape["row"], mesh.shape["feat"]
    rows, width = codes.shape[0] // groups, codes.shape[1] // feats
    n, owned = groups // PLANES, width // groups
    return (
        groups % PLANES == 0
        and 1 < n <= PLANES
        and rows % LANES == 0
        and owned % CHUNK == 0
        and LANES % owned == 0
        and (n * owned) % LANES == 0
    )


def solution(mesh):
    placed = (P("row", "feat"), P("row"), P("row"), P("feat"))

    def run(codes, nodes, labels, weights):
        body = plane_shards if fits(mesh, codes) else shards
        return jax.shard_map(
            body,
            mesh=mesh,
            in_specs=placed,
            out_specs=P(None, ("feat", "row"), None),
            check_vma=False,
        )(codes, nodes, labels, weights)

    return run
```

```python
import functools
import math

import jax
import jax.numpy as jnp
from jax import lax
from jax.experimental import pallas as pl
from jax.experimental.pallas import tpu as pltpu
from jax.sharding import PartitionSpec as P

BINS = 256
NODES = 4
STATS = 2 * NODES
HIGH = 4
LOW = BINS // HIGH
TILE = 16
LANES = 128
AHEAD = 3


def kernel(
    halves,
    inner,
    feats,
    turn,
    given_ref,
    weights_in,
    nodes_in,
    labels_in,
    gain_ref,
    weights_ref,
    nodes_ref,
    labels_ref,
    raw_ref,
    turned_ref,
    margin_ref,
    code_buf,
    margin_buf,
    stat_buf,
    wide_ref,
    high_ref,
    low_ref,
    acc_ref,
    left_ref,
    peer_ref,
    raw_sem,
    own_sem,
    code_send,
    code_recv,
    margin_send,
    margin_recv,
    stat_send,
    stat_recv,
    left_send,
    left_recv,
    take_sem,
):
    parts, size, rows = turned_ref.shape[1:] if turn else given_ref.shape[1:]
    codes_ref = turned_ref if turn else given_ref
    chunks = halves * parts
    batch = math.gcd(inner, 4)
    me_row = lax.axis_index("row")
    me_feat = lax.axis_index("feat")
    me_out = me_row // inner
    me_in = me_row % inner

    def spot(k):
        if inner & (inner - 1):
            return (me_in + k) % inner
        place, bit = 0, 1
        while bit < inner:
            place = place + (me_in // bit + k // bit) % 2 * bit
            bit *= 2
        return place

    def peer(k):
        return me_out * inner + spot(k)

    def across(m):
        return (m + inner // 2) % inner

    partner = ((me_out + 1) % halves) * inner + across(me_in)

    def owner(chunk, k):
        half = (me_out + halves - 1 - chunk // parts) % halves
        place = spot(k)
        return half * inner + jnp.where(chunk < chunks - parts, across(place), place)

    def code_copy(chunk, k):
        return pltpu.make_async_remote_copy(
            src_ref=codes_ref.at[owner(chunk, k), chunk % parts],
            dst_ref=code_buf.at[chunk, k],
            send_sem=code_send.at[chunk, k],
            recv_sem=code_recv.at[chunk, k],
            device_id={"row": peer(k)},
            device_id_type=pl.DeviceIdType.MESH,
        )

    def own_copy(chunk):
        return pltpu.make_async_copy(
            codes_ref.at[owner(chunk, 0), chunk % parts], code_buf.at[chunk, 0], own_sem.at[chunk]
        )

    def margin_copy(k):
        return pltpu.make_async_remote_copy(
            src_ref=margin_ref,
            dst_ref=margin_buf.at[k],
            send_sem=margin_send.at[k],
            recv_sem=margin_recv.at[k],
            device_id={"feat": (me_feat + k) % feats},
            device_id_type=pl.DeviceIdType.MESH,
        )

    def stat_copy(k):
        return pltpu.make_async_remote_copy(
            src_ref=stat_buf.at[0],
            dst_ref=stat_buf.at[k],
            send_sem=stat_send.at[k],
            recv_sem=stat_recv.at[k],
            device_id={"row": peer(k)},
            device_id_type=pl.DeviceIdType.MESH,
        )

    def left_copy(chunk):
        return pltpu.make_async_remote_copy(
            src_ref=left_ref.at[chunk],
            dst_ref=peer_ref.at[chunk],
            send_sem=left_send.at[chunk],
            recv_sem=left_recv.at[chunk],
            device_id={"row": partner},
            device_id_type=pl.DeviceIdType.MESH,
        )

    def each(low, high, body):
        def step(i, carry):
            body(i)
            return carry

        lax.fori_loop(low, high, step, 0)

    takes = [
        pltpu.make_async_copy(source, target, take_sem.at[i])
        for i, (source, target) in enumerate(
            ((weights_in, weights_ref), (nodes_in, nodes_ref), (labels_in, labels_ref))
        )
    ]
    if turn:
        blocks = raw_ref.shape[0]
        near = blocks // halves
        per = LANES // (parts * size)
        first_block = ((me_out + halves - 1) % halves) * (blocks // halves)

        def block_of(t):
            if t < near:
                return (first_block + (t + me_in * 2 // inner * (near // 2)) % near) % blocks
            return (first_block + t) % blocks

        def raw_copy(t):
            column = pl.multiple_of(block_of(t) * LANES, LANES)
            return pltpu.make_async_copy(
                given_ref.at[:, pl.ds(column, LANES)], raw_ref.at[t], raw_sem.at[t]
            )

        raw_copy(0).start()
        for take in takes:
            take.start()
        for t in range(1, blocks):
            raw_copy(t).start()
        part = [jnp.zeros((1, rows), jnp.float32)]

        def turn_block(t):
            raw_copy(t).wait()
            turned = jnp.transpose(raw_ref[t].astype(jnp.float32))
            block = block_of(t)
            turned_ref[pl.ds(block * per, per)] = turned.reshape(per, parts, size, rows)
            centred = (turned - (BINS - 1) / 2.0).astype(jnp.bfloat16)
            weight = weights_ref[:, pl.ds(pl.multiple_of(block * LANES, LANES), LANES)]
            coarse = weight.astype(jnp.bfloat16).astype(jnp.float32)
            rest = weight - coarse
            middle = rest.astype(jnp.bfloat16).astype(jnp.float32)
            line = lax.broadcasted_iota(jnp.int32, (TILE, LANES), 0)
            split = jnp.where(
                line == 0,
                coarse,
                jnp.where(line == 1, middle, jnp.where(line == 2, rest - middle, 0.0)),
            ).astype(jnp.bfloat16)
            product = jnp.dot(split, centred, preferred_element_type=jnp.float32)
            part[0] = part[0] + (product[0:1] + (product[1:2] + product[2:3])) * (2.0 / BINS)

    else:
        for take in takes:
            take.start()
    barrier = pltpu.get_barrier_semaphore()
    each(
        1,
        inner,
        lambda k: pl.semaphore_signal(
            barrier, inc=1, device_id={"row": peer(k)}, device_id_type=pl.DeviceIdType.MESH
        ),
    )
    each(
        1,
        feats,
        lambda k: pl.semaphore_signal(
            barrier,
            inc=1,
            device_id={"feat": (me_feat + k) % feats},
            device_id_type=pl.DeviceIdType.MESH,
        ),
    )
    if halves > 1:
        pl.semaphore_signal(
            barrier, inc=1, device_id={"row": partner}, device_id_type=pl.DeviceIdType.MESH
        )

    def barrier_wait():
        pl.semaphore_wait(barrier, inner - 1 + feats - 1 + halves - 1)

    def send_chunk(chunk):
        own_copy(chunk).start()
        each(1, inner, lambda k: code_copy(chunk, inner - k).start())

    if turn:
        takes[0].wait()
        for t in range(near):
            turn_block(t)
            if t == 0:
                barrier_wait()
            for o in range(per):
                place = (block_of(t) * per + o) % inner
                k = spot(across(place) if halves > 1 else place)

                @pl.when(k == 0)
                def _():
                    own_copy(0).start()

                @pl.when(k > 0)
                def _():
                    code_copy(0, k).start()

        for t in range(near, blocks):
            turn_block(t)
        margin_ref[...] = part[0]
    else:
        takes[0].wait()
        margin_ref[...] = weights_ref[...]
        barrier_wait()
        send_chunk(0)
    each(1, feats, lambda k: margin_copy(k).start())
    margin = margin_ref[...]
    for k in range(1, feats):
        margin_copy(k).wait_recv()
        margin = margin + margin_buf[k]
    takes[1].wait()
    takes[2].wait()
    prob = 1.0 / (1.0 + jnp.exp(-margin))
    grad = prob - labels_ref[...].astype(jnp.float32)
    hess = prob * (1.0 - prob)
    stat_buf[0, 0] = grad
    stat_buf[0, 1] = hess
    stat_buf[0, 2] = nodes_ref[...].astype(jnp.float32)
    each(1, inner, lambda k: stat_copy(k).start())
    for chunk in range(1, AHEAD):
        send_chunk(chunk)

    sub = lax.broadcasted_iota(jnp.int32, (TILE, rows), 0)
    node_id = (sub % NODES).astype(jnp.float32)
    is_grad = sub % STATS < NODES
    high_id = (sub // STATS).astype(jnp.float32).astype(jnp.bfloat16)
    low_id = sub.astype(jnp.float32).astype(jnp.bfloat16)
    zero = jnp.zeros((TILE, rows), jnp.bfloat16)
    one = jnp.ones((TILE, rows), jnp.bfloat16)

    def chunk_step(chunk):
        @pl.when(chunk + AHEAD < chunks)
        def _():
            send_chunk(chunk + AHEAD)

        acc_ref[...] = jnp.zeros_like(acc_ref)
        own_copy(chunk).wait()

        def batch_step(j):
            first = j * batch
            for q in range(batch):
                if q == 0:
                    @pl.when(j > 0)
                    def _():
                        code_copy(chunk, first).wait_recv()
                else:
                    code_copy(chunk, first + q).wait_recv()
                codes = code_buf[chunk, first + q]
                high = jnp.floor(codes * (1.0 / LOW))
                high_ref[q] = high
                low_ref[q] = codes - high * LOW
            @pl.when(chunk == 0)
            def _():
                for q in range(batch):
                    if q == 0:
                        @pl.when(j > 0)
                        def _():
                            stat_copy(first).wait_recv()
                    else:
                        stat_copy(first + q).wait_recv()
                    member = stat_buf[first + q, 2] == node_id
                    wide_ref[first + q] = jnp.where(
                        member,
                        jnp.where(is_grad, stat_buf[first + q, 0], stat_buf[first + q, 1]),
                        0.0,
                    ).astype(jnp.bfloat16)

            stats = [wide_ref[first + q] for q in range(batch)]
            for f in range(size):
                aa, bb = [], []
                for q in range(batch):
                    h = jnp.broadcast_to(high_ref[q, f : f + 1, :], (TILE, rows)).astype(jnp.bfloat16)
                    l = jnp.broadcast_to(low_ref[q, f : f + 1, :], (TILE, rows)).astype(jnp.bfloat16)
                    aa.append(
                        jnp.concatenate(
                            [
                                jnp.where(h == high_id + jnp.bfloat16(i * (TILE // STATS)), stats[q], zero)
                                for i in range(HIGH * STATS // TILE)
                            ],
                            0,
                        )
                    )
                    bb.append(
                        jnp.concatenate(
                            [
                                jnp.where(l <= low_id + jnp.bfloat16(i * TILE), one, zero)
                                for i in range(LOW // TILE)
                            ],
                            0,
                        )
                    )
                acc_ref[f] += lax.dot_general(
                    jnp.concatenate(aa, 1),
                    jnp.concatenate(bb, 1),
                    (((1,), (1,)), ((), ())),
                    preferred_element_type=jnp.float32,
                )

        each(0, inner // batch, batch_step)
        for f in range(size):
            acc = acc_ref[f]
            total = jnp.zeros((STATS, 1), jnp.float32)
            pieces = []
            for h in range(HIGH):
                piece = acc[h * STATS : (h + 1) * STATS] + total
                pieces.append(piece)
                total = piece[:, LOW - 1 : LOW]
            left_ref[chunk, f] = jnp.concatenate(pieces, 1)

        if halves > 1:
            @pl.when(chunk < parts)
            def _():
                left_copy(chunk).start()

    each(0, chunks, chunk_step)

    for c in range(parts):
        if halves > 1:
            left_copy(c).wait_recv()
        lam = 1.0
        paired = size % 2 == 0
        for f in range(0, size, 2 if paired else 1):
            grads, hesses = [], []
            for g in range(f, f + 2 if paired else f + 1):
                left = left_ref[chunks - parts + c, g]
                if halves > 1:
                    left = left + peer_ref[c, g]
                grads.append(left[:NODES])
                hesses.append(left[NODES:])
            gl = jnp.concatenate(grads, 0)
            hl = jnp.concatenate(hesses, 0)
            gt, ht = gl[:, BINS - 1 : BINS], hl[:, BINS - 1 : BINS]
            gain = 0.5 * (
                gl * gl / (hl + lam) + (gt - gl) ** 2 / (ht - hl + lam) - gt * gt / (ht + lam)
            )
            for g in range(len(grads)):
                gain_ref[:, c * size + f + g, :] = gain[g * NODES : (g + 1) * NODES]

    each(1, feats, lambda k: margin_copy(k).wait_send())
    each(1, inner, lambda k: stat_copy(k).wait_send())
    each(0, chunks, lambda c: each(1, inner, lambda k: code_copy(c, k).wait_send()))
    if halves > 1:
        each(0, parts, lambda c: left_copy(c).wait_send())


def shards(codes, nodes, labels, weights):
    row_count, feat_count = codes.shape
    groups = lax.axis_size("row")
    feats = lax.axis_size("feat")
    owned = feat_count // groups
    halves = math.gcd(groups, 2)
    inner = groups // halves
    parts = math.gcd(owned, 4)
    size = owned // parts
    turn = (
        size % 8 == 0
        and LANES % owned == 0
        and feat_count % (LANES * halves) == 0
        and inner & (inner - 1) == 0
    )
    if turn:
        given, vector = codes, weights[None, :]
    else:
        value = (codes.astype(jnp.float32) - (BINS - 1) / 2.0) * (2.0 / BINS)
        vector = jnp.dot(value, weights, precision=lax.Precision.HIGHEST)[None, :]
        given = codes.T.reshape(groups, parts, size, row_count).astype(jnp.float32)
    blocks = feat_count // LANES if turn else 1
    chunks = halves * parts
    batch = math.gcd(inner, 4)
    dma = pltpu.SemaphoreType.DMA
    return pl.pallas_call(
        functools.partial(kernel, halves, inner, feats, turn),
        in_specs=[pl.BlockSpec(memory_space=pl.ANY if turn else pltpu.VMEM)]
        + [pl.BlockSpec(memory_space=pl.ANY)] * 3,
        out_specs=pl.BlockSpec(memory_space=pltpu.VMEM),
        out_shape=pltpu.VMEM((NODES, owned, BINS), jnp.float32),
        scratch_shapes=[
            pltpu.VMEM(vector.shape, jnp.float32),
            pltpu.VMEM((1, row_count), jnp.int32),
            pltpu.VMEM((1, row_count), jnp.int32),
            pltpu.VMEM((blocks, row_count, LANES) if turn else (1, 8, LANES), jnp.int32),
            pltpu.VMEM((groups, parts, size, row_count) if turn else (1, 1, 8, LANES), jnp.float32),
            pltpu.VMEM((1, row_count), jnp.float32),
            pltpu.VMEM((chunks, inner, size, row_count), jnp.float32),
            pltpu.VMEM((feats, 1, row_count), jnp.float32),
            pltpu.VMEM((inner, 3, 1, row_count), jnp.float32),
            pltpu.VMEM((inner, TILE, row_count), jnp.bfloat16),
            pltpu.VMEM((batch, size, row_count), jnp.float32),
            pltpu.VMEM((batch, size, row_count), jnp.float32),
            pltpu.VMEM((size, HIGH * STATS, LOW), jnp.float32),
            pltpu.VMEM((chunks, size, STATS, BINS), jnp.float32),
            pltpu.VMEM((parts, size, STATS, BINS), jnp.float32),
            dma((blocks,)),
            dma((chunks,)),
            dma((chunks, inner)),
            dma((chunks, inner)),
            dma((feats,)),
            dma((feats,)),
            dma((inner,)),
            dma((inner,)),
            dma((parts,)),
            dma((parts,)),
            dma((3,)),
        ],
        compiler_params=pltpu.CompilerParams(collective_id=0, has_side_effects=True),
    )(given, vector, nodes[None, :], labels[None, :])


def solution(mesh):
    placed = (P("row", "feat"), P("row"), P("row"), P("feat"))
    return jax.shard_map(
        shards,
        mesh=mesh,
        in_specs=placed,
        out_specs=P(None, ("feat", "row"), None),
        check_vma=False,
    )
```

```python
import functools
import math

import jax
import jax.numpy as jnp
from jax import lax
from jax.experimental import pallas as pl
from jax.experimental.pallas import tpu as pltpu
from jax.sharding import PartitionSpec as P

BINS = 256
NODES = 4
STATS = 2 * NODES
HIGH = 4
LOW = BINS // HIGH
TILE = 16
LANES = 128
AHEAD = 3


def kernel(
    halves,
    inner,
    feats,
    turn,
    given_ref,
    weights_in,
    nodes_in,
    labels_in,
    gain_ref,
    weights_ref,
    nodes_ref,
    labels_ref,
    raw_ref,
    turned_ref,
    margin_ref,
    code_buf,
    margin_buf,
    stat_buf,
    wide_ref,
    high_ref,
    low_ref,
    acc_ref,
    left_ref,
    peer_ref,
    raw_sem,
    own_sem,
    code_send,
    code_recv,
    margin_send,
    margin_recv,
    stat_send,
    stat_recv,
    left_send,
    left_recv,
    take_sem,
):
    parts, size, rows = turned_ref.shape[1:] if turn else given_ref.shape[1:]
    codes_ref = turned_ref if turn else given_ref
    chunks = halves * parts
    batch = math.gcd(inner, 4)
    me_row = lax.axis_index("row")
    me_feat = lax.axis_index("feat")
    me_out = me_row // inner
    me_in = me_row % inner

    def spot(k):
        if inner & (inner - 1):
            return (me_in + k) % inner
        place, bit = 0, 1
        while bit < inner:
            place = place + (me_in // bit + k // bit) % 2 * bit
            bit *= 2
        return place

    def peer(k):
        return me_out * inner + spot(k)

    def across(m):
        return (m + inner // 2) % inner

    partner = ((me_out + 1) % halves) * inner + across(me_in)

    def owner(chunk, k):
        half = (me_out + halves - 1 - chunk // parts) % halves
        place = spot(k)
        return half * inner + jnp.where(chunk < chunks - parts, across(place), place)

    def code_copy(chunk, k):
        return pltpu.make_async_remote_copy(
            src_ref=codes_ref.at[owner(chunk, k), chunk % parts],
            dst_ref=code_buf.at[chunk, k],
            send_sem=code_send.at[chunk, k],
            recv_sem=code_recv.at[chunk, k],
            device_id={"row": peer(k)},
            device_id_type=pl.DeviceIdType.MESH,
        )

    def own_copy(chunk):
        return pltpu.make_async_copy(
            codes_ref.at[owner(chunk, 0), chunk % parts], code_buf.at[chunk, 0], own_sem.at[chunk]
        )

    def margin_copy(k):
        return pltpu.make_async_remote_copy(
            src_ref=margin_ref,
            dst_ref=margin_buf.at[k],
            send_sem=margin_send.at[k],
            recv_sem=margin_recv.at[k],
            device_id={"feat": (me_feat + k) % feats},
            device_id_type=pl.DeviceIdType.MESH,
        )

    def stat_copy(k):
        return pltpu.make_async_remote_copy(
            src_ref=stat_buf.at[0],
            dst_ref=stat_buf.at[k],
            send_sem=stat_send.at[k],
            recv_sem=stat_recv.at[k],
            device_id={"row": peer(k)},
            device_id_type=pl.DeviceIdType.MESH,
        )

    def left_copy(chunk):
        return pltpu.make_async_remote_copy(
            src_ref=left_ref.at[chunk],
            dst_ref=peer_ref.at[chunk],
            send_sem=left_send.at[chunk],
            recv_sem=left_recv.at[chunk],
            device_id={"row": partner},
            device_id_type=pl.DeviceIdType.MESH,
        )

    def each(low, high, body):
        def step(i, carry):
            body(i)
            return carry

        lax.fori_loop(low, high, step, 0)

    takes = [
        pltpu.make_async_copy(source, target, take_sem.at[i])
        for i, (source, target) in enumerate(
            ((weights_in, weights_ref), (nodes_in, nodes_ref), (labels_in, labels_ref))
        )
    ]
    if turn:
        blocks = raw_ref.shape[0]
        near = blocks // halves
        per = LANES // (parts * size)
        first_block = ((me_out + halves - 1) % halves) * (blocks // halves)

        def block_of(t):
            if t < near:
                return (first_block + (t + me_in * 2 // inner * (near // 2)) % near) % blocks
            return (first_block + t) % blocks

        def raw_copy(t):
            column = pl.multiple_of(block_of(t) * LANES, LANES)
            return pltpu.make_async_copy(
                given_ref.at[:, pl.ds(column, LANES)], raw_ref.at[t], raw_sem.at[t]
            )

        part = [jnp.zeros((1, rows), jnp.float32)]

        def turn_block(t):
            raw_copy(t).wait()
            turned = jnp.transpose(raw_ref[t].astype(jnp.float32))
            block = block_of(t)
            turned_ref[pl.ds(block * per, per)] = turned.reshape(per, parts, size, rows)
            centred = (turned - (BINS - 1) / 2.0).astype(jnp.bfloat16)
            weight = weights_ref[:, pl.ds(pl.multiple_of(block * LANES, LANES), LANES)]
            coarse = weight.astype(jnp.bfloat16).astype(jnp.float32)
            rest = weight - coarse
            middle = rest.astype(jnp.bfloat16).astype(jnp.float32)
            line = lax.broadcasted_iota(jnp.int32, (TILE, LANES), 0)
            split = jnp.where(
                line == 0,
                coarse,
                jnp.where(line == 1, middle, jnp.where(line == 2, rest - middle, 0.0)),
            ).astype(jnp.bfloat16)
            product = jnp.dot(split, centred, preferred_element_type=jnp.float32)
            part[0] = part[0] + (product[0:1] + (product[1:2] + product[2:3])) * (2.0 / BINS)

    barrier = pltpu.get_barrier_semaphore()
    each(
        1,
        inner,
        lambda k: pl.semaphore_signal(
            barrier, inc=1, device_id={"row": peer(k)}, device_id_type=pl.DeviceIdType.MESH
        ),
    )
    each(
        1,
        feats,
        lambda k: pl.semaphore_signal(
            barrier,
            inc=1,
            device_id={"feat": (me_feat + k) % feats},
            device_id_type=pl.DeviceIdType.MESH,
        ),
    )
    if halves > 1:
        pl.semaphore_signal(
            barrier, inc=1, device_id={"row": partner}, device_id_type=pl.DeviceIdType.MESH
        )

    if turn:
        raw_copy(0).start()
        for take in takes:
            take.start()
        for t in range(1, blocks):
            raw_copy(t).start()
    else:
        for take in takes:
            take.start()

    def barrier_wait():
        pl.semaphore_wait(barrier, inner - 1 + feats - 1 + halves - 1)

    def send_chunk(chunk):
        own_copy(chunk).start()
        each(1, inner, lambda k: code_copy(chunk, inner - k).start())

    if turn:
        takes[0].wait()
        for t in range(near):
            turn_block(t)
            if t == 0:
                barrier_wait()
            for o in range(per):
                place = (block_of(t) * per + o) % inner
                k = spot(across(place) if halves > 1 else place)

                @pl.when(k == 0)
                def _():
                    own_copy(0).start()

                @pl.when(k > 0)
                def _():
                    code_copy(0, k).start()

        for t in range(near, blocks):
            turn_block(t)
        margin_ref[...] = part[0]
    else:
        takes[0].wait()
        margin_ref[...] = weights_ref[...]
        barrier_wait()
        send_chunk(0)
    each(1, feats, lambda k: margin_copy(k).start())
    margin = margin_ref[...]
    for k in range(1, feats):
        margin_copy(k).wait_recv()
        margin = margin + margin_buf[k]
    takes[1].wait()
    takes[2].wait()
    prob = 1.0 / (1.0 + jnp.exp(-margin))
    grad = prob - labels_ref[...].astype(jnp.float32)
    hess = prob * (1.0 - prob)
    stat_buf[0, 0] = grad
    stat_buf[0, 1] = hess
    stat_buf[0, 2] = nodes_ref[...].astype(jnp.float32)
    each(1, inner, lambda k: stat_copy(k).start())
    for chunk in range(1, AHEAD):
        send_chunk(chunk)

    sub = lax.broadcasted_iota(jnp.int32, (TILE, rows), 0)
    node_id = (sub % NODES).astype(jnp.float32)
    is_grad = sub % STATS < NODES
    high_id = (sub // STATS).astype(jnp.float32).astype(jnp.bfloat16)
    low_id = sub.astype(jnp.float32).astype(jnp.bfloat16)
    zero = jnp.zeros((TILE, rows), jnp.bfloat16)
    one = jnp.ones((TILE, rows), jnp.bfloat16)

    def chunk_step(chunk):
        @pl.when(chunk + AHEAD < chunks)
        def _():
            send_chunk(chunk + AHEAD)

        acc_ref[...] = jnp.zeros_like(acc_ref)
        own_copy(chunk).wait()

        def batch_step(j):
            first = j * batch
            for q in range(batch):
                if q == 0:
                    @pl.when(j > 0)
                    def _():
                        code_copy(chunk, first).wait_recv()
                else:
                    code_copy(chunk, first + q).wait_recv()
                codes = code_buf[chunk, first + q]
                high = jnp.floor(codes * (1.0 / LOW))
                high_ref[q] = high
                low_ref[q] = codes - high * LOW
            @pl.when(chunk == 0)
            def _():
                for q in range(batch):
                    if q == 0:
                        @pl.when(j > 0)
                        def _():
                            stat_copy(first).wait_recv()
                    else:
                        stat_copy(first + q).wait_recv()
                    member = stat_buf[first + q, 2] == node_id
                    wide_ref[first + q] = jnp.where(
                        member,
                        jnp.where(is_grad, stat_buf[first + q, 0], stat_buf[first + q, 1]),
                        0.0,
                    ).astype(jnp.bfloat16)

            stats = [wide_ref[first + q] for q in range(batch)]
            for f in range(size):
                aa, bb = [], []
                for q in range(batch):
                    h = jnp.broadcast_to(high_ref[q, f : f + 1, :], (TILE, rows)).astype(jnp.bfloat16)
                    l = jnp.broadcast_to(low_ref[q, f : f + 1, :], (TILE, rows)).astype(jnp.bfloat16)
                    aa.append(
                        jnp.concatenate(
                            [
                                jnp.where(h == high_id + jnp.bfloat16(i * (TILE // STATS)), stats[q], zero)
                                for i in range(HIGH * STATS // TILE)
                            ],
                            0,
                        )
                    )
                    bb.append(
                        jnp.concatenate(
                            [
                                jnp.where(l <= low_id + jnp.bfloat16(i * TILE), one, zero)
                                for i in range(LOW // TILE)
                            ],
                            0,
                        )
                    )
                acc_ref[f] += lax.dot_general(
                    jnp.concatenate(aa, 1),
                    jnp.concatenate(bb, 1),
                    (((1,), (1,)), ((), ())),
                    preferred_element_type=jnp.float32,
                )

        each(0, inner // batch, batch_step)
        for f in range(size):
            acc = acc_ref[f]
            total = jnp.zeros((STATS, 1), jnp.float32)
            pieces = []
            for h in range(HIGH):
                piece = acc[h * STATS : (h + 1) * STATS] + total
                pieces.append(piece)
                total = piece[:, LOW - 1 : LOW]
            left_ref[chunk, f] = jnp.concatenate(pieces, 1)

        if halves > 1:
            @pl.when(chunk < parts)
            def _():
                left_copy(chunk).start()

    each(0, chunks, chunk_step)

    for c in range(parts):
        if halves > 1:
            left_copy(c).wait_recv()
        lam = 1.0
        paired = size % 2 == 0
        for f in range(0, size, 2 if paired else 1):
            grads, hesses = [], []
            for g in range(f, f + 2 if paired else f + 1):
                left = left_ref[chunks - parts + c, g]
                if halves > 1:
                    left = left + peer_ref[c, g]
                grads.append(left[:NODES])
                hesses.append(left[NODES:])
            gl = jnp.concatenate(grads, 0)
            hl = jnp.concatenate(hesses, 0)
            gt, ht = gl[:, BINS - 1 : BINS], hl[:, BINS - 1 : BINS]
            gain = 0.5 * (
                gl * gl / (hl + lam) + (gt - gl) ** 2 / (ht - hl + lam) - gt * gt / (ht + lam)
            )
            for g in range(len(grads)):
                gain_ref[:, c * size + f + g, :] = gain[g * NODES : (g + 1) * NODES]

    each(1, feats, lambda k: margin_copy(k).wait_send())
    each(1, inner, lambda k: stat_copy(k).wait_send())
    each(0, chunks, lambda c: each(1, inner, lambda k: code_copy(c, k).wait_send()))
    if halves > 1:
        each(0, parts, lambda c: left_copy(c).wait_send())


def shards(codes, nodes, labels, weights):
    row_count, feat_count = codes.shape
    groups = lax.axis_size("row")
    feats = lax.axis_size("feat")
    owned = feat_count // groups
    halves = math.gcd(groups, 2)
    inner = groups // halves
    parts = math.gcd(owned, 4)
    size = owned // parts
    turn = (
        size % 8 == 0
        and LANES % owned == 0
        and feat_count % (LANES * halves) == 0
        and inner & (inner - 1) == 0
    )
    if turn:
        given, vector = codes, weights[None, :]
    else:
        value = (codes.astype(jnp.float32) - (BINS - 1) / 2.0) * (2.0 / BINS)
        vector = jnp.dot(value, weights, precision=lax.Precision.HIGHEST)[None, :]
        given = codes.T.reshape(groups, parts, size, row_count).astype(jnp.float32)
    blocks = feat_count // LANES if turn else 1
    chunks = halves * parts
    batch = math.gcd(inner, 4)
    dma = pltpu.SemaphoreType.DMA
    return pl.pallas_call(
        functools.partial(kernel, halves, inner, feats, turn),
        in_specs=[pl.BlockSpec(memory_space=pl.ANY if turn else pltpu.VMEM)]
        + [pl.BlockSpec(memory_space=pl.ANY)] * 3,
        out_specs=pl.BlockSpec(memory_space=pltpu.VMEM),
        out_shape=pltpu.VMEM((NODES, owned, BINS), jnp.float32),
        scratch_shapes=[
            pltpu.VMEM(vector.shape, jnp.float32),
            pltpu.VMEM((1, row_count), jnp.int32),
            pltpu.VMEM((1, row_count), jnp.int32),
            pltpu.VMEM((blocks, row_count, LANES) if turn else (1, 8, LANES), jnp.int32),
            pltpu.VMEM((groups, parts, size, row_count) if turn else (1, 1, 8, LANES), jnp.float32),
            pltpu.VMEM((1, row_count), jnp.float32),
            pltpu.VMEM((chunks, inner, size, row_count), jnp.float32),
            pltpu.VMEM((feats, 1, row_count), jnp.float32),
            pltpu.VMEM((inner, 3, 1, row_count), jnp.float32),
            pltpu.VMEM((inner, TILE, row_count), jnp.bfloat16),
            pltpu.VMEM((batch, size, row_count), jnp.float32),
            pltpu.VMEM((batch, size, row_count), jnp.float32),
            pltpu.VMEM((size, HIGH * STATS, LOW), jnp.float32),
            pltpu.VMEM((chunks, size, STATS, BINS), jnp.float32),
            pltpu.VMEM((parts, size, STATS, BINS), jnp.float32),
            dma((blocks,)),
            dma((chunks,)),
            dma((chunks, inner)),
            dma((chunks, inner)),
            dma((feats,)),
            dma((feats,)),
            dma((inner,)),
            dma((inner,)),
            dma((parts,)),
            dma((parts,)),
            dma((3,)),
        ],
        compiler_params=pltpu.CompilerParams(collective_id=0, has_side_effects=True),
    )(given, vector, nodes[None, :], labels[None, :])


def solution(mesh):
    placed = (P("row", "feat"), P("row"), P("row"), P("feat"))
    return jax.shard_map(
        shards,
        mesh=mesh,
        in_specs=placed,
        out_specs=P(None, ("feat", "row"), None),
        check_vma=False,
    )
```

```python
import functools
import math

import jax
import jax.numpy as jnp
from jax import lax
from jax.experimental import pallas as pl
from jax.experimental.pallas import tpu as pltpu
from jax.sharding import PartitionSpec as P

BINS = 256
NODES = 4
STATS = 2 * NODES
HIGH = 4
LOW = BINS // HIGH
TILE = 16
LANES = 128
AHEAD = 3


def kernel(
    halves,
    inner,
    feats,
    turn,
    given_ref,
    weights_in,
    nodes_in,
    labels_in,
    gain_ref,
    weights_ref,
    nodes_ref,
    labels_ref,
    raw_ref,
    turned_ref,
    margin_ref,
    code_buf,
    margin_buf,
    stat_buf,
    wide_ref,
    high_ref,
    low_ref,
    acc_ref,
    left_ref,
    peer_ref,
    raw_sem,
    own_sem,
    code_send,
    code_recv,
    margin_send,
    margin_recv,
    stat_send,
    stat_recv,
    left_send,
    left_recv,
    take_sem,
):
    parts, size, rows = turned_ref.shape[1:] if turn else given_ref.shape[1:]
    codes_ref = turned_ref if turn else given_ref
    chunks = halves * parts
    batch = math.gcd(inner, 4)
    me_row = lax.axis_index("row")
    me_feat = lax.axis_index("feat")
    me_out = me_row // inner
    me_in = me_row % inner

    def spot(k):
        if inner & (inner - 1):
            return (me_in + k) % inner
        place, bit = 0, 1
        while bit < inner:
            place = place + (me_in // bit + k // bit) % 2 * bit
            bit *= 2
        return place

    def peer(k):
        return me_out * inner + spot(k)

    def across(m):
        return (m + inner // 2) % inner

    partner = ((me_out + 1) % halves) * inner + across(me_in)

    def owner(chunk, k):
        half = (me_out + halves - 1 - chunk // parts) % halves
        place = spot(k)
        return half * inner + jnp.where(chunk < chunks - parts, across(place), place)

    def code_copy(chunk, k):
        return pltpu.make_async_remote_copy(
            src_ref=codes_ref.at[owner(chunk, k), chunk % parts],
            dst_ref=code_buf.at[chunk, k],
            send_sem=code_send.at[chunk, k],
            recv_sem=code_recv.at[chunk, k],
            device_id={"row": peer(k)},
            device_id_type=pl.DeviceIdType.MESH,
        )

    def own_copy(chunk):
        return pltpu.make_async_copy(
            codes_ref.at[owner(chunk, 0), chunk % parts], code_buf.at[chunk, 0], own_sem.at[chunk]
        )

    def margin_copy(k):
        return pltpu.make_async_remote_copy(
            src_ref=margin_ref,
            dst_ref=margin_buf.at[k],
            send_sem=margin_send.at[k],
            recv_sem=margin_recv.at[k],
            device_id={"feat": (me_feat + k) % feats},
            device_id_type=pl.DeviceIdType.MESH,
        )

    def stat_copy(k):
        return pltpu.make_async_remote_copy(
            src_ref=stat_buf.at[0],
            dst_ref=stat_buf.at[k],
            send_sem=stat_send.at[k],
            recv_sem=stat_recv.at[k],
            device_id={"row": peer(k)},
            device_id_type=pl.DeviceIdType.MESH,
        )

    def left_copy(chunk):
        return pltpu.make_async_remote_copy(
            src_ref=left_ref.at[chunk],
            dst_ref=peer_ref.at[chunk],
            send_sem=left_send.at[chunk],
            recv_sem=left_recv.at[chunk],
            device_id={"row": partner},
            device_id_type=pl.DeviceIdType.MESH,
        )

    def each(low, high, body):
        def step(i, carry):
            body(i)
            return carry

        lax.fori_loop(low, high, step, 0)

    takes = [
        pltpu.make_async_copy(source, target, take_sem.at[i])
        for i, (source, target) in enumerate(
            ((weights_in, weights_ref), (nodes_in, nodes_ref), (labels_in, labels_ref))
        )
    ]
    if turn:
        blocks = raw_ref.shape[0]
        near = blocks // halves
        per = LANES // (parts * size)
        first_block = ((me_out + halves - 1) % halves) * (blocks // halves)

        def block_of(t):
            if t < near:
                return (first_block + (t + me_in * 2 // inner * (near // 2)) % near) % blocks
            return (first_block + t) % blocks

        def raw_copy(t):
            column = pl.multiple_of(block_of(t) * LANES, LANES)
            return pltpu.make_async_copy(
                given_ref.at[:, pl.ds(column, LANES)], raw_ref.at[t], raw_sem.at[t]
            )

        part = [jnp.zeros((1, rows), jnp.float32)]

        def turn_block(t):
            raw_copy(t).wait()
            turned = jnp.transpose(raw_ref[t].astype(jnp.float32))
            block = block_of(t)
            turned_ref[pl.ds(block * per, per)] = turned.reshape(per, parts, size, rows)
            centred = (turned - (BINS - 1) / 2.0).astype(jnp.bfloat16)
            weight = weights_ref[:, pl.ds(pl.multiple_of(block * LANES, LANES), LANES)]
            coarse = weight.astype(jnp.bfloat16).astype(jnp.float32)
            rest = weight - coarse
            middle = rest.astype(jnp.bfloat16).astype(jnp.float32)
            line = lax.broadcasted_iota(jnp.int32, (TILE, LANES), 0)
            split = jnp.where(
                line == 0,
                coarse,
                jnp.where(line == 1, middle, jnp.where(line == 2, rest - middle, 0.0)),
            ).astype(jnp.bfloat16)
            product = jnp.dot(split, centred, preferred_element_type=jnp.float32)
            part[0] = part[0] + (product[0:1] + (product[1:2] + product[2:3])) * (2.0 / BINS)

    barrier = pltpu.get_barrier_semaphore()
    each(
        1,
        inner,
        lambda k: pl.semaphore_signal(
            barrier, inc=1, device_id={"row": peer(k)}, device_id_type=pl.DeviceIdType.MESH
        ),
    )
    each(
        1,
        feats,
        lambda k: pl.semaphore_signal(
            barrier,
            inc=1,
            device_id={"feat": (me_feat + k) % feats},
            device_id_type=pl.DeviceIdType.MESH,
        ),
    )
    if halves > 1:
        pl.semaphore_signal(
            barrier, inc=1, device_id={"row": partner}, device_id_type=pl.DeviceIdType.MESH
        )

    if turn:
        raw_copy(0).start()
        for take in takes:
            take.start()
        for t in range(1, blocks):
            raw_copy(t).start()
    else:
        for take in takes:
            take.start()

    def barrier_wait():
        pl.semaphore_wait(barrier, inner - 1 + feats - 1 + halves - 1)

    def send_chunk(chunk):
        own_copy(chunk).start()
        each(1, inner, lambda k: code_copy(chunk, inner - k).start())

    if turn:
        takes[0].wait()
        for t in range(near):
            turn_block(t)
            if t == 0:
                barrier_wait()
            for o in range(per):
                place = (block_of(t) * per + o) % inner
                k = spot(across(place) if halves > 1 else place)

                @pl.when(k == 0)
                def _():
                    own_copy(0).start()

                @pl.when(k > 0)
                def _():
                    code_copy(0, k).start()

        for t in range(near, blocks):
            turn_block(t)
        margin_ref[...] = part[0]
    else:
        takes[0].wait()
        margin_ref[...] = weights_ref[...]
        barrier_wait()
        send_chunk(0)
    each(1, feats, lambda k: margin_copy(k).start())
    margin = margin_ref[...]
    for k in range(1, feats):
        margin_copy(k).wait_recv()
        margin = margin + margin_buf[k]
    takes[1].wait()
    takes[2].wait()
    prob = 1.0 / (1.0 + jnp.exp(-margin))
    grad = prob - labels_ref[...].astype(jnp.float32)
    hess = prob * (1.0 - prob)
    stat_buf[0, 0] = grad
    stat_buf[0, 1] = hess
    stat_buf[0, 2] = nodes_ref[...].astype(jnp.float32)
    each(1, inner, lambda k: stat_copy(k).start())
    for chunk in range(1, AHEAD):
        send_chunk(chunk)

    sub = lax.broadcasted_iota(jnp.int32, (TILE, rows), 0)
    node_id = (sub % NODES).astype(jnp.float32)
    is_grad = sub % STATS < NODES
    high_id = (sub // STATS).astype(jnp.float32).astype(jnp.bfloat16)
    low_id = sub.astype(jnp.float32).astype(jnp.bfloat16)
    zero = jnp.zeros((TILE, rows), jnp.bfloat16)
    one = jnp.ones((TILE, rows), jnp.bfloat16)

    def chunk_step(chunk):
        @pl.when(chunk + AHEAD < chunks)
        def _():
            send_chunk(chunk + AHEAD)

        own_copy(chunk).wait()

        def batch_step(j):
            first = j * batch
            for q in range(batch):
                if q == 0:
                    @pl.when(j > 0)
                    def _():
                        code_copy(chunk, first).wait_recv()
                else:
                    code_copy(chunk, first + q).wait_recv()
                codes = code_buf[chunk, first + q]
                high = jnp.floor(codes * (1.0 / LOW))
                high_ref[q] = high
                low_ref[q] = codes - high * LOW
            @pl.when(chunk == 0)
            def _():
                for q in range(batch):
                    if q == 0:
                        @pl.when(j > 0)
                        def _():
                            stat_copy(first).wait_recv()
                    else:
                        stat_copy(first + q).wait_recv()
                    member = stat_buf[first + q, 2] == node_id
                    wide_ref[first + q] = jnp.where(
                        member,
                        jnp.where(is_grad, stat_buf[first + q, 0], stat_buf[first + q, 1]),
                        0.0,
                    ).astype(jnp.bfloat16)

            stats = [wide_ref[first + q] for q in range(batch)]
            for f in range(size):
                aa, bb = [], []
                for q in range(batch):
                    h = jnp.broadcast_to(high_ref[q, f : f + 1, :], (TILE, rows)).astype(jnp.bfloat16)
                    l = jnp.broadcast_to(low_ref[q, f : f + 1, :], (TILE, rows)).astype(jnp.bfloat16)
                    aa.append(
                        jnp.concatenate(
                            [
                                jnp.where(h == high_id + jnp.bfloat16(i * (TILE // STATS)), stats[q], zero)
                                for i in range(HIGH * STATS // TILE)
                            ],
                            0,
                        )
                    )
                    bb.append(
                        jnp.concatenate(
                            [
                                jnp.where(l <= low_id + jnp.bfloat16(i * TILE), one, zero)
                                for i in range(LOW // TILE)
                            ],
                            0,
                        )
                    )
                acc_ref[f] = jnp.where(j == 0, 0.0, acc_ref[f]) + lax.dot_general(
                    jnp.concatenate(aa, 1),
                    jnp.concatenate(bb, 1),
                    (((1,), (1,)), ((), ())),
                    preferred_element_type=jnp.float32,
                )

        each(0, inner // batch, batch_step)
        for f in range(size):
            acc = acc_ref[f]
            total = jnp.zeros((STATS, 1), jnp.float32)
            pieces = []
            for h in range(HIGH):
                piece = acc[h * STATS : (h + 1) * STATS] + total
                pieces.append(piece)
                total = piece[:, LOW - 1 : LOW]
            left_ref[chunk, f] = jnp.concatenate(pieces, 1)

        if halves > 1:
            @pl.when(chunk < parts)
            def _():
                left_copy(chunk).start()

    each(0, chunks, chunk_step)

    for c in range(parts):
        if halves > 1:
            left_copy(c).wait_recv()
        lam = 1.0
        paired = size % 2 == 0
        for f in range(0, size, 2 if paired else 1):
            grads, hesses = [], []
            for g in range(f, f + 2 if paired else f + 1):
                left = left_ref[chunks - parts + c, g]
                if halves > 1:
                    left = left + peer_ref[c, g]
                grads.append(left[:NODES])
                hesses.append(left[NODES:])
            gl = jnp.concatenate(grads, 0)
            hl = jnp.concatenate(hesses, 0)
            gt, ht = gl[:, BINS - 1 : BINS], hl[:, BINS - 1 : BINS]
            gain = 0.5 * (
                gl * gl / (hl + lam) + (gt - gl) ** 2 / (ht - hl + lam) - gt * gt / (ht + lam)
            )
            for g in range(len(grads)):
                gain_ref[:, c * size + f + g, :] = gain[g * NODES : (g + 1) * NODES]

    each(1, feats, lambda k: margin_copy(k).wait_send())
    each(1, inner, lambda k: stat_copy(k).wait_send())
    each(0, chunks, lambda c: each(1, inner, lambda k: code_copy(c, k).wait_send()))
    if halves > 1:
        each(0, parts, lambda c: left_copy(c).wait_send())


def shards(codes, nodes, labels, weights):
    row_count, feat_count = codes.shape
    groups = lax.axis_size("row")
    feats = lax.axis_size("feat")
    owned = feat_count // groups
    halves = math.gcd(groups, 2)
    inner = groups // halves
    parts = math.gcd(owned, 4)
    size = owned // parts
    turn = (
        size % 8 == 0
        and LANES % owned == 0
        and feat_count % (LANES * halves) == 0
        and inner & (inner - 1) == 0
    )
    if turn:
        given, vector = codes, weights[None, :]
    else:
        value = (codes.astype(jnp.float32) - (BINS - 1) / 2.0) * (2.0 / BINS)
        vector = jnp.dot(value, weights, precision=lax.Precision.HIGHEST)[None, :]
        given = codes.T.reshape(groups, parts, size, row_count).astype(jnp.float32)
    blocks = feat_count // LANES if turn else 1
    chunks = halves * parts
    batch = math.gcd(inner, 4)
    dma = pltpu.SemaphoreType.DMA
    return pl.pallas_call(
        functools.partial(kernel, halves, inner, feats, turn),
        in_specs=[pl.BlockSpec(memory_space=pl.ANY if turn else pltpu.VMEM)]
        + [pl.BlockSpec(memory_space=pl.ANY)] * 3,
        out_specs=pl.BlockSpec(memory_space=pltpu.VMEM),
        out_shape=pltpu.VMEM((NODES, owned, BINS), jnp.float32),
        scratch_shapes=[
            pltpu.VMEM(vector.shape, jnp.float32),
            pltpu.VMEM((1, row_count), jnp.int32),
            pltpu.VMEM((1, row_count), jnp.int32),
            pltpu.VMEM((blocks, row_count, LANES) if turn else (1, 8, LANES), jnp.int32),
            pltpu.VMEM((groups, parts, size, row_count) if turn else (1, 1, 8, LANES), jnp.float32),
            pltpu.VMEM((1, row_count), jnp.float32),
            pltpu.VMEM((chunks, inner, size, row_count), jnp.float32),
            pltpu.VMEM((feats, 1, row_count), jnp.float32),
            pltpu.VMEM((inner, 3, 1, row_count), jnp.float32),
            pltpu.VMEM((inner, TILE, row_count), jnp.bfloat16),
            pltpu.VMEM((batch, size, row_count), jnp.float32),
            pltpu.VMEM((batch, size, row_count), jnp.float32),
            pltpu.VMEM((size, HIGH * STATS, LOW), jnp.float32),
            pltpu.VMEM((chunks, size, STATS, BINS), jnp.float32),
            pltpu.VMEM((parts, size, STATS, BINS), jnp.float32),
            dma((blocks,)),
            dma((chunks,)),
            dma((chunks, inner)),
            dma((chunks, inner)),
            dma((feats,)),
            dma((feats,)),
            dma((inner,)),
            dma((inner,)),
            dma((parts,)),
            dma((parts,)),
            dma((3,)),
        ],
        compiler_params=pltpu.CompilerParams(collective_id=0, has_side_effects=True),
    )(given, vector, nodes[None, :], labels[None, :])


def solution(mesh):
    placed = (P("row", "feat"), P("row"), P("row"), P("feat"))
    return jax.shard_map(
        shards,
        mesh=mesh,
        in_specs=placed,
        out_specs=P(None, ("feat", "row"), None),
        check_vma=False,
    )
```
